256 devices in a mesh: lev: 8 (over z_lo, y), hor: 32 (over z_hi, x, core).
Axes of the slice: x: 4, y: 4, z: 8 (z_hi: 4, z_lo: 2; z = z_hi * 2 + z_lo), core: 2. Of those that a mesh axis runs over, the one named last changes fastest.
Arguments:
- heat_field: float32 [256, 512, 512], P('lev', 'hor'), may hold values from -6 to 6
- saline_field: float32 [256, 512, 512], P('lev', 'hor'), may hold values from -6 to 6
- updraft_speed: float32 [256, 512, 512], P('lev', 'hor'), may hold values from -3 to 3
- heat_mixing_rates: float32 [256], P('lev'), may hold values from 0.05 to 1
- saline_mixing_rates: float32 [256], P('lev'), may hold values from 0.05 to 1
- cross_mixing_rates: float32 [256], P('lev'), may hold values from 0.2 to 1
Outputs:
- updated_heat_field: float32 [256, 512, 512], P('lev', 'hor')
- salt_out: float32 [256, 512, 512], P('lev', 'hor')
The draws below stay inside these ranges and needn't reach their ends.
All inputs are finite; a program needn't handle non-finite values.
Results may differ from the reference program's by a relative error of at most 0.000073.
Values sent between devices are 32-bit elements; how exact they have to be, the bound alone decides.
No kernel may reach another device: no remote copies, remote signals or barrier semaphores. Data moves between devices by JAX's collectives and lax.ppermute only.
A program may use at most 128 MiB of HBM per device.

```python
import math
import jax
import jax.numpy as jnp
from jax import lax

GRID_WIDTH_EAST = 512
GRID_WIDTH_NORTH = 512
DEPTH_LAYERS = 256


def shard_levels(own_key, shape, shards, least, largest):
    factor_of = 1.0
    for axis_at, blocks in shards:
        draws = jax.random.uniform(jax.random.fold_in(jax.random.fold_in(own_key, 6), axis_at), (blocks,), jnp.float32, least / len(shards), largest / len(shards))
        factor_of = factor_of * jnp.repeat(jnp.exp(draws), shape[axis_at] // blocks).reshape((-1,) + (1,) * (len(shape) - 1 - axis_at))
    return factor_of


def gaussian(key, shape, scale, reach, split=(), kind=jnp.bfloat16):
    entries = scale * jax.random.normal(key, shape, jnp.float32)
    if split:
        entries = entries * shard_levels(key, shape, split, -0.22, 0.18)
    return jnp.clip(entries, -reach, reach).astype(kind)


def setup_inputs(seed: int = 0) -> dict:
    key_list = jax.random.split(jax.random.key(seed), 7)
    heat_field = gaussian(key_list[0], (DEPTH_LAYERS, GRID_WIDTH_EAST, GRID_WIDTH_NORTH), 1.0, 6.0, ((0, 8), (1, 32)), jnp.float32)
    saline_field = gaussian(key_list[1], (DEPTH_LAYERS, GRID_WIDTH_EAST, GRID_WIDTH_NORTH), 1.0, 6.0, ((0, 8), (1, 32)), jnp.float32)
    updraft_speed = gaussian(key_list[2], (DEPTH_LAYERS, GRID_WIDTH_EAST, GRID_WIDTH_NORTH), 0.5, 3.0, ((0, 8), (1, 32)), jnp.float32)
    heat_mixing_rates = jnp.clip(jnp.exp(math.log(1.0) - 2.9957323 * jax.random.uniform(key_list[3], (DEPTH_LAYERS,), jnp.float32) ** shard_levels(key_list[3], (DEPTH_LAYERS,), ((0, 8),), -0.2, 0.2)), 0.05, 1.0)
    saline_mixing_rates = jnp.clip(jnp.exp(math.log(1.0) - 2.9957323 * jax.random.uniform(key_list[4], (DEPTH_LAYERS,), jnp.float32) ** shard_levels(key_list[4], (DEPTH_LAYERS,), ((0, 8),), -0.2, 0.2)), 0.05, 1.0)
    cross_mixing_rates = jnp.clip(jnp.exp(math.log(1.0) - 1.609438 * jax.random.uniform(key_list[5], (DEPTH_LAYERS,), jnp.float32) ** shard_levels(key_list[5], (DEPTH_LAYERS,), ((0, 8),), -0.2, 0.2)), 0.2, 1.0)
    return dict(heat_field=heat_field, saline_field=saline_field, updraft_speed=updraft_speed, heat_mixing_rates=heat_mixing_rates, saline_mixing_rates=saline_mixing_rates, cross_mixing_rates=cross_mixing_rates)


def signed_waves(length):
    waves = jnp.arange(length)
    return jnp.where(waves < length // 2, waves, waves - length)


def layer_fourier_modes(pieces):
    temp_level, salt_level, diff_temp, diff_salt, cross_rate = pieces
    wave_x = signed_waves(GRID_WIDTH_EAST).astype(temp_level.dtype)
    wave_y = signed_waves(GRID_WIDTH_NORTH).astype(temp_level.dtype)
    modulus = (wave_x[:, None] * wave_x[:, None] + wave_y[None, :] * wave_y[None, :]) / ((GRID_WIDTH_EAST / 2.0) * (GRID_WIDTH_EAST / 2.0))
    fourier_temp = jnp.fft.fft2(temp_level)
    fourier_salt = jnp.fft.fft2(salt_level)
    diag_temp = 1.0 + diff_temp * modulus
    diag_salt = 1.0 + diff_salt * modulus
    cross_term = cross_rate * modulus
    determinant = diag_temp * diag_salt + cross_term * cross_term
    new_temp = (diag_salt * fourier_temp - cross_term * fourier_salt) / determinant
    new_salt = (diag_temp * fourier_salt + cross_term * fourier_temp) / determinant
    back_temp = jnp.real(jnp.fft.ifft2(new_temp)).astype(temp_level.dtype)
    back_salt = jnp.real(jnp.fft.ifft2(new_salt)).astype(temp_level.dtype)
    return back_temp, back_salt


def reference(heat_field, saline_field, updraft_speed, heat_mixing_rates, saline_mixing_rates, cross_mixing_rates):
    filtered_heat_field, filtered_saline_field = lax.map(layer_fourier_modes, (heat_field, saline_field, heat_mixing_rates, saline_mixing_rates, cross_mixing_rates))
    interface_flow = 0.5 * (updraft_speed[:-1] + updraft_speed[1:]) + 0.5 * 0.5 * ((filtered_heat_field[:-1] + filtered_heat_field[1:]) - (filtered_saline_field[:-1] + filtered_saline_field[1:]))
    upward_flow = jnp.maximum(interface_flow, 0.0)
    downward_flow = jnp.minimum(interface_flow, 0.0)
    heat_transport = upward_flow * filtered_heat_field[:-1] + downward_flow * filtered_heat_field[1:]
    flux_salt = upward_flow * filtered_saline_field[:-1] + downward_flow * filtered_saline_field[1:]
    zero_face = jnp.zeros_like(heat_transport[:1])
    heat_transport = jnp.concatenate([zero_face, heat_transport, zero_face], axis=0)
    flux_salt = jnp.concatenate([zero_face, flux_salt, zero_face], axis=0)
    updated_heat_field = filtered_heat_field - 0.25 * (heat_transport[1:] - heat_transport[:-1])
    salt_out = filtered_saline_field - 0.25 * (flux_salt[1:] - flux_salt[:-1])
    return updated_heat_field, salt_out
```

```python
import functools
import math

import jax
import jax.numpy as jnp
import numpy as np
from jax import lax
from jax.experimental import pallas as pl
from jax.experimental.pallas import tpu as pltpu
from jax.sharding import PartitionSpec as P

buoyancy = 0.5
advective_number = 0.25


def real_basis(length):
    half = length // 2
    points = np.arange(half)
    tables, waves = [], []
    for parity in (0, 1):
        cos_waves = np.arange(parity, half + 1, 2)
        sin_waves = np.array([k for k in cos_waves if 0 < k < half])
        rows = []
        for k in cos_waves:
            weight = math.sqrt((1.0 if k in (0, half) else 2.0) / length)
            rows.append(weight * np.cos(2.0 * math.pi / length * ((k * points) % length)))
        for k in sin_waves:
            rows.append(math.sqrt(2.0 / length) * np.sin(2.0 * math.pi / length * ((k * points) % length)))
        tables.append(np.stack(rows))
        waves.append(np.concatenate([cos_waves, sin_waves]))
    return tables, waves


def parts_of(table):
    kind = np.dtype(jnp.bfloat16)
    high = table.astype(kind)
    return high, (table - high.astype(np.float64)).astype(kind)


def split(value):
    high = value.astype(jnp.bfloat16)
    low = (value - high.astype(jnp.float32)).astype(jnp.bfloat16)
    return high, low


def dot(left, right):
    return jnp.dot(left, right, preferred_element_type=jnp.float32)


def right_product(value, table_high, table_low):
    high, low = split(value)
    return dot(high, table_high) + dot(low, table_high) + dot(high, table_low)


def left_product(table_high, table_low, value):
    high, low = split(value)
    return dot(table_high, high) + dot(table_low, high) + dot(table_high, low)


def spectral_kernel(rt_ref, rs_ref, rc_ref, x_ref, tab_ref, sq_ref, sqt_ref, out_ref):
    length = x_ref.shape[-1]
    half = length // 2
    level = lax.axis_index("hor")
    rate_t, rate_s, rate_c = rt_ref[level], rs_ref[level], rc_ref[level]

    def table(parity, transposed, low):
        return tab_ref[parity * 4 + transposed * 2 + low]

    def folded(field):
        value = x_ref[:, field].reshape(length, length)
        rows = (value[:half] + value[half:], value[:half] - value[half:])
        return [[r[:, :half] + r[:, half:], r[:, :half] - r[:, half:]] for r in rows]

    planes = [folded(0), folded(1)]
    inner = {}
    for q in (0, 1):
        stacked = jnp.concatenate([planes[f][p][q] for f in (0, 1) for p in (0, 1)], axis=0)
        product = right_product(stacked, table(q, 1, 0), table(q, 1, 1))
        for f in (0, 1):
            for p in (0, 1):
                at = (2 * f + p) * half
                inner[f, p, q] = product[at : at + half]
    back = {}
    for p in (0, 1):
        stacked = jnp.concatenate([inner[f, p, q] for f in (0, 1) for q in (0, 1)], axis=1)
        product = left_product(table(p, 0, 0), table(p, 0, 1), stacked)
        temp, salt = product[:, :length], product[:, length:]
        modulus = (sq_ref[:, p : p + 1] + sqt_ref[...]) / ((length / 2.0) * (length / 2.0))
        diag_temp = 1.0 + rate_t * modulus
        diag_salt = 1.0 + rate_s * modulus
        cross = rate_c * modulus
        determinant = diag_temp * diag_salt + cross * cross
        new_temp = (diag_salt * temp - cross * salt) / determinant
        new_salt = (diag_temp * salt + cross * temp) / determinant
        product = left_product(
            table(p, 1, 0), table(p, 1, 1), jnp.concatenate([new_temp, new_salt], axis=1)
        )
        for f in (0, 1):
            for q in (0, 1):
                at = (2 * f + q) * half
                back[f, p, q] = product[:, at : at + half]
    result = {}
    for q in (0, 1):
        stacked = jnp.concatenate([back[f, p, q] for f in (0, 1) for p in (0, 1)], axis=0)
        product = right_product(stacked, table(q, 0, 0), table(q, 0, 1))
        for f in (0, 1):
            for p in (0, 1):
                at = (2 * f + p) * half
                result[f, p, q] = product[at : at + half]
    blocks = x_ref.shape[0] // 2
    shape = (blocks,) + x_ref.shape[2:3] + (half,)
    for f in (0, 1):
        rows = [(result[f, p, 0] + result[f, p, 1], result[f, p, 0] - result[f, p, 1]) for p in (0, 1)]
        for side in (0, 1):
            columns = slice(side * half, (side + 1) * half)
            out_ref[:blocks, f, :, columns] = (rows[0][side] + rows[1][side]).reshape(shape)
            out_ref[blocks:, f, :, columns] = (rows[0][side] - rows[1][side]).reshape(shape)


def spectral_step(x, rate_t, rate_s, rate_c):
    length = x.shape[-1]
    tables, waves = real_basis(length)
    stack = []
    for table in tables:
        for oriented in (table, table.T):
            stack.extend(parts_of(oriented))
    squares = np.stack([w.astype(np.float32) ** 2 for w in waves], axis=1)
    vmem = pl.BlockSpec(memory_space=pltpu.VMEM)
    smem = pl.BlockSpec(memory_space=pltpu.SMEM)
    return pl.pallas_call(
        spectral_kernel,
        out_shape=jax.ShapeDtypeStruct(x.shape, jnp.float32),
        in_specs=[smem] * 3 + [vmem] * 4,
        out_specs=vmem,
        compiler_params=pltpu.CompilerParams(vmem_limit_bytes=40 << 20),
        name="spectral",
    )(
        rate_t,
        rate_s,
        rate_c,
        x,
        jnp.asarray(np.stack(stack)),
        jnp.asarray(squares),
        jnp.asarray(np.concatenate([squares[:, 0], squares[:, 1]])[None, :]),
    )


def flux_kernel(u_ref, w_ref, low_ref, high_ref, wlow_ref, whigh_ref, t_out, s_out):
    levels = u_ref.shape[0]
    block = lax.axis_index("lev")
    last = lax.axis_size("lev") - 1

    def face(lt, ls, lw, ut, us, uw):
        flow = 0.5 * (lw + uw) + buoyancy * 0.5 * ((lt + ut) - (ls + us))
        up = jnp.maximum(flow, 0.0)
        down = jnp.minimum(flow, 0.0)
        return up * lt + down * ut, up * ls + down * us

    at = (u_ref[0, 0], u_ref[0, 1], w_ref[0])
    below = face(low_ref[0], low_ref[1], wlow_ref[...], *at)
    open_low = block > 0
    below = tuple(jnp.where(open_low, b, 0.0) for b in below)
    for level in range(levels):
        if level + 1 < levels:
            nxt = (u_ref[level + 1, 0], u_ref[level + 1, 1], w_ref[level + 1])
            above = face(*at, *nxt)
        else:
            nxt = None
            above = face(*at, high_ref[0], high_ref[1], whigh_ref[...])
            above = tuple(jnp.where(block < last, a, 0.0) for a in above)
        t_out[level] = at[0] - advective_number * (above[0] - below[0])
        s_out[level] = at[1] - advective_number * (above[1] - below[1])
        at, below = nxt, above


def shards(heat, saline, updraft, rate_t, rate_s, rate_c):
    count = lax.axis_size("lev")
    upward = [(i, i + 1) for i in range(count - 1)]
    downward = [(i + 1, i) for i in range(count - 1)]
    w_low = lax.ppermute(updraft[-1], "lev", upward)
    w_high = lax.ppermute(updraft[0], "lev", downward)
    both = jnp.stack([heat, saline], axis=1)
    whole = lax.all_to_all(both, "hor", split_axis=0, concat_axis=0, tiled=True)
    solved = spectral_step(whole, rate_t, rate_s, rate_c)
    filtered = lax.all_to_all(solved, "hor", split_axis=0, concat_axis=0, tiled=True)
    low = lax.ppermute(filtered[-1], "lev", upward)
    high = lax.ppermute(filtered[0], "lev", downward)
    vmem = pl.BlockSpec(memory_space=pltpu.VMEM)
    shape = jax.ShapeDtypeStruct(heat.shape, jnp.float32)
    return pl.pallas_call(
        flux_kernel,
        out_shape=(shape, shape),
        in_specs=[vmem] * 6,
        out_specs=(vmem, vmem),
        name="flux",
    )(filtered, updraft, low, high, w_low, w_high)


def solution(mesh):
    field = P("lev", "hor", None)
    return jax.shard_map(
        shards,
        mesh=mesh,
        in_specs=(field,) * 3 + (P("lev"),) * 3,
        out_specs=(field, field),
        check_vma=False,
    )
```

```python
import functools
import math

import jax
import jax.numpy as jnp
import numpy as np
from jax import lax
from jax.experimental import pallas as pl
from jax.experimental.pallas import tpu as pltpu
from jax.sharding import PartitionSpec as P


buoyancy = 0.5
advective_number = 0.25


def real_basis(length):
    half = length // 2
    points = np.arange(half)
    tables, waves = [], []
    for parity in (0, 1):
        cos_waves = np.arange(parity, half + 1, 2)
        sin_waves = np.array([k for k in cos_waves if 0 < k < half])
        rows = []
        for k in cos_waves:
            weight = math.sqrt((1.0 if k in (0, half) else 2.0) / length)
            rows.append(weight * np.cos(2.0 * math.pi / length * ((k * points) % length)))
        for k in sin_waves:
            rows.append(math.sqrt(2.0 / length) * np.sin(2.0 * math.pi / length * ((k * points) % length)))
        tables.append(np.stack(rows))
        waves.append(np.concatenate([cos_waves, sin_waves]))
    return tables, waves


def parts_of(table):
    kind = np.dtype(jnp.bfloat16)
    high = table.astype(kind)
    return high, (table - high.astype(np.float64)).astype(kind)


def split(value):
    high = value.astype(jnp.bfloat16)
    low = (value - high.astype(jnp.float32)).astype(jnp.bfloat16)
    return high, low


def dot(left, right):
    return jnp.dot(left, right, preferred_element_type=jnp.float32)


def right_product(value, table_high, table_low):
    high, low = split(value)
    return dot(high, table_high) + dot(low, table_high) + dot(high, table_low)


def left_product(table_high, table_low, value):
    high, low = split(value)
    return dot(table_high, high) + dot(table_low, high) + dot(table_high, low)


def position():
    at = lax.axis_index("hor")
    return at // 8, (at // 2) % 4, at % 2


def block_to(place, step, near):
    z, x, c = place
    return ((z + step) % 4) * 8 + ((x + near // 2) % 4) * 2 + (c + near % 2) % 2


def block_from(place, step, near):
    z, x, c = place
    return ((z + 4 - step) % 4) * 8 + ((x + 4 - near // 2) % 4) * 2 + (c + near % 2) % 2


def fold_kernel(heat_ref, salt_ref, *refs):
    half = heat_ref.shape[-1] // 2
    by_step, by_near = refs[:4], refs[4:]
    place = position()
    for step in range(4):
        for near in range(8):
            level = block_to(place, step, near)
            for f, ref in enumerate((heat_ref, salt_ref)):
                value = ref[level]
                by_step[step][near, f] = value[:, :half] + value[:, half:]
                by_near[near][step, f] = value[:, :half] - value[:, half:]


def repack_kernel(*refs):
    groups = 32 // refs[0].shape[0]
    for i in range(groups):
        for j in range(32 // groups):
            refs[groups + j][i] = refs[i][j]


def gathered(refs, out_ref):
    place = position()
    for i, ref in enumerate(refs):
        for j in range(ref.shape[0]):
            step, near = (i, j) if len(refs) == 4 else (j, i)
            out_ref[block_from(place, step, near)] = ref[j]


def unpack_kernel(*refs):
    pieces, (out_ref, first_ref, last_ref) = refs[:-3], refs[-3:]
    gathered(pieces, out_ref)
    first_ref[...] = out_ref[0]
    last_ref[...] = out_ref[out_ref.shape[0] - 1]


def transformed(parity, rates, x_ref, tab_ref, sq_ref, sqt_ref):
    half = x_ref.shape[-1]
    length = 2 * half
    rate_t, rate_s, rate_c = rates

    def table(which, transposed, low):
        return tab_ref[which * 4 + transposed * 2 + low]

    planes = []
    for f in (0, 1):
        value = x_ref[:, f].reshape(length, half)
        planes += [value[:half] + value[half:], value[:half] - value[half:]]
    inner = right_product(
        jnp.concatenate(planes, axis=0), table(parity, 1, 0), table(parity, 1, 1)
    )
    back = {}
    for p in (0, 1):
        stacked = jnp.concatenate(
            [inner[(2 * f + p) * half : (2 * f + p + 1) * half] for f in (0, 1)], axis=1
        )
        product = left_product(table(p, 0, 0), table(p, 0, 1), stacked)
        temp, salt = product[:, :half], product[:, half:]
        modulus = (sq_ref[:, p : p + 1] + sqt_ref[parity : parity + 1]) / (
            (length / 2.0) * (length / 2.0)
        )
        diag_temp = 1.0 + rate_t * modulus
        diag_salt = 1.0 + rate_s * modulus
        cross = rate_c * modulus
        determinant = diag_temp * diag_salt + cross * cross
        new_temp = (diag_salt * temp - cross * salt) / determinant
        new_salt = (diag_temp * salt + cross * temp) / determinant
        product = left_product(
            table(p, 1, 0), table(p, 1, 1), jnp.concatenate([new_temp, new_salt], axis=1)
        )
        for f in (0, 1):
            back[f, p] = product[:, f * half : (f + 1) * half]
    stacked = jnp.concatenate([back[f, p] for f in (0, 1) for p in (0, 1)], axis=0)
    result = right_product(stacked, table(parity, 0, 0), table(parity, 0, 1))
    out = []
    for f in (0, 1):
        plus = result[2 * f * half : (2 * f + 1) * half]
        minus = result[(2 * f + 1) * half : (2 * f + 2) * half]
        out.append((plus + minus, plus - minus))
    return out


def store_rows(out_ref, result):
    blocks, _, rows, half = out_ref.shape
    for f in (0, 1):
        for side in (0, 1):
            at = slice(side * blocks // 2, (side + 1) * blocks // 2)
            out_ref[at, f] = result[f][side].reshape(blocks // 2, rows, half)


def spectral_kernel(parity, rt_ref, rs_ref, rc_ref, tab_ref, sq_ref, sqt_ref, *refs):
    inputs, outs, held = (refs[:8], refs[8:12], refs[12]) if parity == 0 else (refs[:4], refs[4:12], refs[12])
    gathered(inputs, held)
    level = lax.axis_index("hor")
    rates = (rt_ref[level], rs_ref[level], rc_ref[level])
    store_rows(held, transformed(parity, rates, held, tab_ref, sq_ref, sqt_ref))
    place = position()
    for step in range(4):
        for near in range(8):
            block = held[block_to(place, step, near)]
            if parity == 0:
                outs[step][near] = block
            else:
                outs[near][step] = block


def flux_kernel(
    even_ref, odd_ref, w_ref, elow_ref, ehigh_ref, olow_ref, ohigh_ref, wlow_ref, whigh_ref, t_out, s_out
):
    levels = w_ref.shape[0]
    block = lax.axis_index("lev")
    last = lax.axis_size("lev") - 1

    def unfolded(even, odd):
        return tuple(
            jnp.concatenate([even[f] + odd[f], even[f] - odd[f]], axis=-1) for f in (0, 1)
        )

    def at_level(level):
        return unfolded(even_ref[level], odd_ref[level]) + (w_ref[level],)

    def face(lower, upper):
        lt, ls, lw = lower
        ut, us, uw = upper
        flow = 0.5 * (lw + uw) + buoyancy * 0.5 * ((lt + ut) - (ls + us))
        up = jnp.maximum(flow, 0.0)
        down = jnp.minimum(flow, 0.0)
        return up * lt + down * ut, up * ls + down * us

    at = at_level(0)
    below = face(unfolded(elow_ref[...], olow_ref[...]) + (wlow_ref[...],), at)
    below = tuple(jnp.where(block > 0, b, 0.0) for b in below)
    for level in range(levels):
        if level + 1 < levels:
            nxt = at_level(level + 1)
            above = face(at, nxt)
        else:
            nxt = unfolded(ehigh_ref[...], ohigh_ref[...]) + (whigh_ref[...],)
            above = tuple(jnp.where(block < last, a, 0.0) for a in face(at, nxt))
        t_out[level] = at[0] - advective_number * (above[0] - below[0])
        s_out[level] = at[1] - advective_number * (above[1] - below[1])
        at, below = nxt, above


def constants(length):
    tables, waves = real_basis(length)
    stack = []
    for table in tables:
        for oriented in (table, table.T):
            stack.extend(parts_of(oriented))
    squares = np.stack([w.astype(np.float32) ** 2 for w in waves], axis=1)
    return np.stack(stack), squares, np.ascontiguousarray(squares.T)


vmem = pl.BlockSpec(memory_space=pltpu.VMEM)
smem = pl.BlockSpec(memory_space=pltpu.SMEM)


def call(kernel, outs, *args, smem_args=0, scratch=(), flops=0):
    moved = sum(math.prod(a.shape) * 4 for a in args) + sum(math.prod(o.shape) * 4 for o in outs)
    return pl.pallas_call(
        kernel,
        out_shape=tuple(outs),
        in_specs=[smem] * smem_args + [vmem] * (len(args) - smem_args),
        out_specs=(vmem,) * len(outs),
        scratch_shapes=scratch,
        compiler_params=pltpu.CompilerParams(vmem_limit_bytes=24 << 20),
        cost_estimate=pl.CostEstimate(flops=flops, bytes_accessed=moved, transcendentals=0),
    )(*args)


def step_of(heat, saline, updraft, rate_t, rate_s, rate_c):
    levels, rows, length = heat.shape
    half = length // 2
    f32 = jnp.float32
    by_plane = jax.ShapeDtypeStruct((8, 2, rows, half), f32)
    by_near = jax.ShapeDtypeStruct((4, 2, rows, half), f32)
    whole = jax.ShapeDtypeStruct((levels, 2, rows, half), f32)
    edge = jax.ShapeDtypeStruct((2, rows, half), f32)
    table, squares, squares_t = (jnp.asarray(c) for c in constants(length))
    shared = (rate_t, rate_s, rate_c, table, squares, squares_t)
    flops = 3 * 16 * 2 * half**3

    def along_z(pieces):
        out = [pieces[0]]
        for step in (1, 2, 3):
            pairs = [(h, (h + 8 * step) % 32) for h in range(32)]
            out.append(lax.ppermute(pieces[step], "hor", pairs))
        return out

    def in_plane(pieces):
        out = [pieces[0]]
        for near in range(1, 8):
            pairs = [
                (z * 8 + x * 2 + c, z * 8 + (x + near // 2) % 4 * 2 + (c + near) % 2)
                for z in range(4)
                for x in range(4)
                for c in range(2)
            ]
            out.append(lax.ppermute(pieces[near], "hor", pairs))
        return out

    def halo(first, last):
        return lax.ppermute(last, "lev", upward), lax.ppermute(first, "lev", downward)

    def kernel(body, outs, *args, **kwargs):
        return call(body, outs, *args, **kwargs)

    def repacked(pieces):
        outs = [by_near] * 8 if len(pieces) == 4 else [by_plane] * 4
        return kernel(repack_kernel, outs, *pieces)

    def solved(parity, pieces):
        outs = [by_plane] * 4 if parity == 0 else [by_near] * 8
        return kernel(
            functools.partial(spectral_kernel, parity), outs, *shared, *pieces,
            smem_args=3, flops=flops, scratch=[pltpu.VMEM(whole.shape, f32)],
        )

    count = lax.axis_size("lev")
    upward = [(i, i + 1) for i in range(count - 1)]
    downward = [(i + 1, i) for i in range(count - 1)]

    folded = kernel(fold_kernel, [by_plane] * 4 + [by_near] * 8, heat, saline)
    even, odd = folded[:4], folded[4:]
    even = along_z(even)
    odd = in_plane(odd)
    w_halo = halo(updraft[0], updraft[-1])
    odd = along_z(repacked(odd))
    even = in_plane(repacked(even))
    even = along_z(solved(0, even))
    odd = in_plane(solved(1, odd))
    odd = along_z(repacked(odd))
    even = in_plane(repacked(even))
    even, *even_ends = kernel(unpack_kernel, [whole, edge, edge], *even)
    even_halo = halo(*even_ends)
    odd, *odd_ends = kernel(unpack_kernel, [whole, edge, edge], *odd)
    odd_halo = halo(*odd_ends)
    field = jax.ShapeDtypeStruct(heat.shape, f32)
    return kernel(flux_kernel, [field, field], even, odd, updraft, *even_halo, *odd_halo, *w_halo)


def solution(mesh):
    field = P("lev", "hor", None)
    return jax.shard_map(
        step_of,
        mesh=mesh,
        in_specs=(field,) * 3 + (P("lev"),) * 3,
        out_specs=(field, field),
        check_vma=False,
    )
```

```python
import functools
import math

import jax
import jax.numpy as jnp
import numpy as np
from jax import lax
from jax.experimental import pallas as pl
from jax.experimental.pallas import tpu as pltpu
from jax.sharding import PartitionSpec as P


buoyancy = 0.5
advective_number = 0.25


def real_basis(length):
    half = length // 2
    points = np.arange(half)
    tables, waves = [], []
    for parity in (0, 1):
        cos_waves = np.arange(parity, half + 1, 2)
        sin_waves = np.array([k for k in cos_waves if 0 < k < half])
        rows = []
        for k in cos_waves:
            weight = math.sqrt((1.0 if k in (0, half) else 2.0) / length)
            rows.append(weight * np.cos(2.0 * math.pi / length * ((k * points) % length)))
        for k in sin_waves:
            rows.append(math.sqrt(2.0 / length) * np.sin(2.0 * math.pi / length * ((k * points) % length)))
        tables.append(np.stack(rows))
        waves.append(np.concatenate([cos_waves, sin_waves]))
    return tables, waves


def parts_of(table):
    kind = np.dtype(jnp.bfloat16)
    high = table.astype(kind)
    return high, (table - high.astype(np.float64)).astype(kind)


def split(value):
    high = value.astype(jnp.bfloat16)
    low = (value - high.astype(jnp.float32)).astype(jnp.bfloat16)
    return high, low


def dot(left, right):
    return jnp.dot(left, right, preferred_element_type=jnp.float32)


def right_product(value, table_high, table_low):
    high, low = split(value)
    return dot(high, table_high) + dot(low, table_high) + dot(high, table_low)


def left_product(table_high, table_low, value):
    high, low = split(value)
    return dot(table_high, high) + dot(table_low, high) + dot(table_high, low)


def position():
    at = lax.axis_index("hor")
    return at // 8, (at // 2) % 4, at % 2


def block_to(place, step, near):
    z, x, c = place
    return ((z + step) % 4) * 8 + ((x + near // 2) % 4) * 2 + (c + near % 2) % 2


def block_from(place, step, near):
    z, x, c = place
    return ((z + 4 - step) % 4) * 8 + ((x + 4 - near // 2) % 4) * 2 + (c + near % 2) % 2


def fold_kernel(heat_ref, salt_ref, *refs):
    half = heat_ref.shape[-1] // 2
    by_step, by_near = refs[:4], refs[4:]
    place = position()
    for step in range(4):
        for near in range(8):
            level = block_to(place, step, near)
            for f, ref in enumerate((heat_ref, salt_ref)):
                value = ref[level]
                by_step[step][near, f] = value[:, :half] + value[:, half:]
                by_near[near][step, f] = value[:, :half] - value[:, half:]


def repack_kernel(*refs):
    groups = 32 // refs[0].shape[0]
    for i in range(groups):
        for j in range(32 // groups):
            refs[groups + j][i] = refs[i][j]


def gathered(refs, out_ref):
    place = position()
    for i, ref in enumerate(refs):
        for j in range(ref.shape[0]):
            step, near = (i, j) if len(refs) == 4 else (j, i)
            out_ref[block_from(place, step, near)] = ref[j]


def unpack_kernel(*refs):
    pieces, (out_ref, first_ref, last_ref) = refs[:-3], refs[-3:]
    gathered(pieces, out_ref)
    first_ref[...] = out_ref[0]
    last_ref[...] = out_ref[out_ref.shape[0] - 1]


def unpack_with_speed_kernel(w_first_ref, w_last_ref, *refs):
    pieces, (out_ref, first_ref, last_ref) = refs[:-3], refs[-3:]
    gathered(pieces, out_ref)
    half = out_ref.shape[-1]
    for edge_ref, w_ref, level in ((first_ref, w_first_ref, 0), (last_ref, w_last_ref, out_ref.shape[0] - 1)):
        edge_ref[:2] = out_ref[level]
        edge_ref[2] = w_ref[0, :, :half]
        edge_ref[3] = w_ref[0, :, half:]


def transformed(parity, rates, x_ref, tab_ref, sq_ref, sqt_ref):
    half = x_ref.shape[-1]
    length = 2 * half
    rate_t, rate_s, rate_c = rates

    def table(which, transposed, low):
        return tab_ref[which * 4 + transposed * 2 + low]

    planes = []
    for f in (0, 1):
        value = x_ref[:, f].reshape(length, half)
        planes += [value[:half] + value[half:], value[:half] - value[half:]]
    inner = right_product(
        jnp.concatenate(planes, axis=0), table(parity, 1, 0), table(parity, 1, 1)
    )
    back = {}
    for p in (0, 1):
        stacked = jnp.concatenate(
            [inner[(2 * f + p) * half : (2 * f + p + 1) * half] for f in (0, 1)], axis=1
        )
        product = left_product(table(p, 0, 0), table(p, 0, 1), stacked)
        temp, salt = product[:, :half], product[:, half:]
        modulus = (sq_ref[:, p : p + 1] + sqt_ref[parity : parity + 1]) / (
            (length / 2.0) * (length / 2.0)
        )
        diag_temp = 1.0 + rate_t * modulus
        diag_salt = 1.0 + rate_s * modulus
        cross = rate_c * modulus
        determinant = diag_temp * diag_salt + cross * cross
        new_temp = (diag_salt * temp - cross * salt) / determinant
        new_salt = (diag_temp * salt + cross * temp) / determinant
        product = left_product(
            table(p, 1, 0), table(p, 1, 1), jnp.concatenate([new_temp, new_salt], axis=1)
        )
        for f in (0, 1):
            back[f, p] = product[:, f * half : (f + 1) * half]
    stacked = jnp.concatenate([back[f, p] for f in (0, 1) for p in (0, 1)], axis=0)
    result = right_product(stacked, table(parity, 0, 0), table(parity, 0, 1))
    out = []
    for f in (0, 1):
        plus = result[2 * f * half : (2 * f + 1) * half]
        minus = result[(2 * f + 1) * half : (2 * f + 2) * half]
        out.append((plus + minus, plus - minus))
    return out


def store_rows(out_ref, result):
    blocks, _, rows, half = out_ref.shape
    for f in (0, 1):
        for side in (0, 1):
            at = slice(side * blocks // 2, (side + 1) * blocks // 2)
            out_ref[at, f] = result[f][side].reshape(blocks // 2, rows, half)


def spectral_kernel(parity, rt_ref, rs_ref, rc_ref, tab_ref, sq_ref, sqt_ref, *refs):
    inputs, outs, held = (refs[:8], refs[8:12], refs[12]) if parity == 0 else (refs[:4], refs[4:12], refs[12])
    gathered(inputs, held)
    level = lax.axis_index("hor")
    rates = (rt_ref[level], rs_ref[level], rc_ref[level])
    store_rows(held, transformed(parity, rates, held, tab_ref, sq_ref, sqt_ref))
    place = position()
    for step in range(4):
        for near in range(8):
            block = held[block_to(place, step, near)]
            if parity == 0:
                outs[step][near] = block
            else:
                outs[near][step] = block


def unfolded(even, odd):
    return tuple(jnp.concatenate([even[f] + odd[f], even[f] - odd[f]], axis=-1) for f in (0, 1))


def face(lower, upper):
    lt, ls, lw = lower
    ut, us, uw = upper
    flow = 0.5 * (lw + uw) + buoyancy * 0.5 * ((lt + ut) - (ls + us))
    up = jnp.maximum(flow, 0.0)
    down = jnp.minimum(flow, 0.0)
    return up * lt + down * ut, up * ls + down * us


def inner_flux_kernel(even_ref, odd_ref, w_ref, t_out, s_out, t_first, s_first, t_last, s_last):
    levels = w_ref.shape[0]

    def at_level(level):
        return unfolded(even_ref[level], odd_ref[level]) + (w_ref[level],)

    at = at_level(0)
    t_first[0], s_first[0] = at[0], at[1]
    below = (jnp.zeros_like(at[0]),) * 2

    def body(level, carried):
        at, below = carried[:3], carried[3:]
        nxt = at_level(level + 1)
        above = face(at, nxt)
        t_out[level] = at[0] - advective_number * (above[0] - below[0])
        s_out[level] = at[1] - advective_number * (above[1] - below[1])
        return nxt + above

    carried = at + below
    carried = lax.fori_loop(0, levels - 1, body, carried)
    at, below = carried[:3], carried[3:]
    t_last[0], s_last[0] = at[0], at[1]
    t_out[levels - 1] = at[0] + advective_number * below[0]
    s_out[levels - 1] = at[1] + advective_number * below[1]


def outer_flux_kernel(
    t_ref, s_ref, tf_ref, sf_ref, tl_ref, sl_ref, wf_ref, wl_ref, elow, ehigh, olow, ohigh, t_out, s_out
):
    block = lax.axis_index("lev")
    edge = pl.program_id(0)

    def speed(ref):
        return jnp.concatenate([ref[2], ref[3]], axis=-1)

    @pl.when(edge == 0)
    def _():
        other = unfolded(elow[...], olow[...]) + (speed(elow),)
        flux = face(other, (tf_ref[0], sf_ref[0], wf_ref[0]))
        t_out[0] = t_ref[0] + advective_number * jnp.where(block > 0, flux[0], 0.0)
        s_out[0] = s_ref[0] + advective_number * jnp.where(block > 0, flux[1], 0.0)

    @pl.when(edge == 1)
    def _():
        other = unfolded(ehigh[...], ohigh[...]) + (speed(ehigh),)
        flux = face((tl_ref[0], sl_ref[0], wl_ref[0]), other)
        is_open = block < lax.axis_size("lev") - 1
        t_out[0] = t_ref[0] - advective_number * jnp.where(is_open, flux[0], 0.0)
        s_out[0] = s_ref[0] - advective_number * jnp.where(is_open, flux[1], 0.0)


def constants(length):
    tables, waves = real_basis(length)
    stack = []
    for table in tables:
        for oriented in (table, table.T):
            stack.extend(parts_of(oriented))
    squares = np.stack([w.astype(np.float32) ** 2 for w in waves], axis=1)
    return np.stack(stack), squares, np.ascontiguousarray(squares.T)


vmem = pl.BlockSpec(memory_space=pltpu.VMEM)
smem = pl.BlockSpec(memory_space=pltpu.SMEM)


def call(kernel, outs, *args, smem_args=0, scratch=(), flops=0, specs=None, grid=()):
    moved = sum(math.prod(a.shape) * 4 for a in args) + sum(math.prod(o.shape) * 4 for o in outs)
    return pl.pallas_call(
        kernel,
        out_shape=tuple(outs),
        grid=grid,
        in_specs=specs or [smem] * smem_args + [vmem] * (len(args) - smem_args),
        out_specs=(vmem,) * len(outs),
        scratch_shapes=scratch,
        compiler_params=pltpu.CompilerParams(vmem_limit_bytes=24 << 20),
        cost_estimate=pl.CostEstimate(flops=flops, bytes_accessed=moved, transcendentals=0),
    )(*args)


def step_of(heat, saline, updraft, rate_t, rate_s, rate_c):
    levels, rows, length = heat.shape
    half = length // 2
    f32 = jnp.float32
    by_plane = jax.ShapeDtypeStruct((8, 2, rows, half), f32)
    by_near = jax.ShapeDtypeStruct((4, 2, rows, half), f32)
    whole = jax.ShapeDtypeStruct((levels, 2, rows, half), f32)
    edge = jax.ShapeDtypeStruct((2, rows, half), f32)
    table, squares, squares_t = (jnp.asarray(c) for c in constants(length))
    shared = (rate_t, rate_s, rate_c, table, squares, squares_t)
    flops = 3 * 16 * 2 * half**3

    def along_z(pieces):
        out = [pieces[0]]
        for step in (1, 2, 3):
            pairs = [(h, (h + 8 * step) % 32) for h in range(32)]
            out.append(lax.ppermute(pieces[step], "hor", pairs))
        return out

    def in_plane(pieces):
        out = [pieces[0]]
        for near in range(1, 8):
            pairs = [
                (z * 8 + x * 2 + c, z * 8 + (x + near // 2) % 4 * 2 + (c + near) % 2)
                for z in range(4)
                for x in range(4)
                for c in range(2)
            ]
            out.append(lax.ppermute(pieces[near], "hor", pairs))
        return out

    def halo(first, last):
        return lax.ppermute(last, "lev", upward), lax.ppermute(first, "lev", downward)

    def kernel(body, outs, *args, **kwargs):
        return call(body, outs, *args, **kwargs)

    def repacked(pieces):
        outs = [by_near] * 8 if len(pieces) == 4 else [by_plane] * 4
        return kernel(repack_kernel, outs, *pieces)

    def solved(parity, pieces):
        outs = [by_plane] * 4 if parity == 0 else [by_near] * 8
        return kernel(
            functools.partial(spectral_kernel, parity), outs, *shared, *pieces,
            smem_args=3, flops=flops, scratch=[pltpu.VMEM(whole.shape, f32)],
        )

    count = lax.axis_size("lev")
    upward = [(i, i + 1) for i in range(count - 1)]
    downward = [(i + 1, i) for i in range(count - 1)]

    folded = kernel(fold_kernel, [by_plane] * 4 + [by_near] * 8, heat, saline)
    even, odd = folded[:4], folded[4:]
    even = along_z(even)
    odd = in_plane(odd)
    odd = along_z(repacked(odd))
    even = in_plane(repacked(even))
    even = along_z(solved(0, even))
    odd = in_plane(solved(1, odd))
    odd = along_z(repacked(odd))
    even = in_plane(repacked(even))
    first_level = pl.BlockSpec((1, rows, length), lambda *_: (0, 0, 0))
    last_level = pl.BlockSpec((1, rows, length), lambda *_: (levels - 1, 0, 0))
    edge_with_speed = jax.ShapeDtypeStruct((4, rows, half), f32)
    even, *even_ends = kernel(
        unpack_with_speed_kernel, [whole, edge_with_speed, edge_with_speed], updraft, updraft, *even,
        specs=[first_level, last_level] + [vmem] * 8, grid=(1,),
    )
    even_halo = halo(*even_ends)
    odd, *odd_ends = kernel(unpack_kernel, [whole, edge, edge], *odd)
    odd_halo = halo(*odd_ends)
    field = jax.ShapeDtypeStruct(heat.shape, f32)
    one = jax.ShapeDtypeStruct((1, rows, length), f32)
    temp, salt, *ends = kernel(inner_flux_kernel, [field, field, one, one, one, one], even, odd, updraft)
    both_ends = pl.BlockSpec((1, rows, length), lambda i: (i * (levels - 1), 0, 0))
    return pl.pallas_call(
        outer_flux_kernel,
        grid=(2,),
        out_shape=(field, field),
        in_specs=[both_ends] * 2 + [vmem] * 4 + [
            pl.BlockSpec((1, rows, length), lambda i: (0, 0, 0)),
            pl.BlockSpec((1, rows, length), lambda i: (levels - 1, 0, 0)),
        ] + [vmem] * 4,
        out_specs=(both_ends, both_ends),
        input_output_aliases={0: 0, 1: 1},
        name="outer",
    )(temp, salt, *ends, updraft, updraft, *even_halo, *odd_halo)


def solution(mesh):
    field = P("lev", "hor", None)
    return jax.shard_map(
        step_of,
        mesh=mesh,
        in_specs=(field,) * 3 + (P("lev"),) * 3,
        out_specs=(field, field),
        check_vma=False,
    )
```

```python
import functools
import math

import jax
import jax.numpy as jnp
import numpy as np
from jax import lax
from jax.experimental import pallas as pl
from jax.experimental.pallas import tpu as pltpu
from jax.sharding import PartitionSpec as P


buoyancy = 0.5
advective_number = 0.25


STEPS = (1, 3, 2)


def real_basis(length):
    half = length // 2
    points = np.arange(half)
    tables, waves = [], []
    for parity in (0, 1):
        cos_waves = np.arange(parity, half + 1, 2)
        sin_waves = np.array([k for k in cos_waves if 0 < k < half])
        rows = []
        for k in cos_waves:
            weight = math.sqrt((1.0 if k in (0, half) else 2.0) / length)
            rows.append(weight * np.cos(2.0 * math.pi / length * ((k * points) % length)))
        for k in sin_waves:
            rows.append(math.sqrt(2.0 / length) * np.sin(2.0 * math.pi / length * ((k * points) % length)))
        tables.append(np.stack(rows))
        waves.append(np.concatenate([cos_waves, sin_waves]))
    return tables, waves


def parts_of(table):
    kind = np.dtype(jnp.bfloat16)
    high = table.astype(kind)
    return high, (table - high.astype(np.float64)).astype(kind)


def split(value):
    high = value.astype(jnp.bfloat16)
    low = (value - high.astype(jnp.float32)).astype(jnp.bfloat16)
    return high, low


def dot(left, right):
    return jnp.dot(left, right, preferred_element_type=jnp.float32)


def right_product(value, table_high, table_low):
    high, low = split(value)
    return dot(high, table_high) + dot(low, table_high) + dot(high, table_low)


def left_product(table_high, table_low, value):
    high, low = split(value)
    return dot(table_high, high) + dot(table_low, high) + dot(table_high, low)


def position():
    at = lax.axis_index("hor")
    return at // 8, (at // 2) % 4, at % 2


def block_to(place, step, near):
    z, x, c = place
    return ((z + step) % 4) * 8 + ((x + near // 2) % 4) * 2 + (c + near % 2) % 2


def block_from(place, step, near):
    z, x, c = place
    return ((z + 4 - step) % 4) * 8 + ((x + 4 - near // 2) % 4) * 2 + (c + near % 2) % 2


def fold_kernel(heat_ref, salt_ref, *refs):
    half = heat_ref.shape[-1] // 2
    by_step, by_near, held, arrived = refs[:4], refs[4:12], refs[12], refs[13]
    place = position()
    copies = []
    for step in STEPS + (0,):
        rows = pl.ds((place[0] + step) % 4 * 8, 8)
        copies.append(
            [
                pltpu.make_async_copy(ref.at[rows], held.at[f, step], arrived.at[f, step])
                for f, ref in enumerate((heat_ref, salt_ref))
            ]
        )
        for copy in copies[-1]:
            copy.start()
    for step, pair in zip(STEPS + (0,), copies):
        for f in (0, 1):
            pair[f].wait()
            for near in range(8):
                value = held[f, step, block_to(place, 0, near) - place[0] * 8]
                by_step[step][near, f] = value[:, :half] + value[:, half:]
                by_near[near][step, f] = value[:, :half] - value[:, half:]


def repack_kernel(*refs):
    groups = 32 // refs[0].shape[0]
    for i in range(groups):
        for j in range(32 // groups):
            refs[groups + j][i] = refs[i][j]


def gathered(refs, out_ref):
    place = position()
    for i, ref in enumerate(refs):
        for j in range(ref.shape[0]):
            step, near = (i, j) if len(refs) == 4 else (j, i)
            out_ref[block_from(place, step, near)] = ref[j]


def unpack_kernel(w_first_ref, w_last_ref, *refs):
    even_ref, odd_ref, first_ref, last_ref = refs[12:]
    gathered(refs[:8], even_ref)
    gathered(refs[8:12], odd_ref)
    half = even_ref.shape[-1]
    for edge_ref, w_ref, level in ((first_ref, w_first_ref, 0), (last_ref, w_last_ref, even_ref.shape[0] - 1)):
        edge_ref[:2] = even_ref[level]
        edge_ref[2:4] = odd_ref[level]
        edge_ref[4] = w_ref[0, :, :half]
        edge_ref[5] = w_ref[0, :, half:]


def transformed(parity, rates, x_ref, tab_ref, sq_ref, sqt_ref):
    half = x_ref.shape[-1]
    length = 2 * half
    rate_t, rate_s, rate_c = rates

    def table(which, transposed, low):
        return tab_ref[which * 4 + transposed * 2 + low]

    planes = []
    for f in (0, 1):
        value = x_ref[:, f].reshape(length, half)
        planes += [value[:half] + value[half:], value[:half] - value[half:]]
    inner = right_product(
        jnp.concatenate(planes, axis=0), table(parity, 1, 0), table(parity, 1, 1)
    )
    back = {}
    for p in (0, 1):
        stacked = jnp.concatenate(
            [inner[(2 * f + p) * half : (2 * f + p + 1) * half] for f in (0, 1)], axis=1
        )
        product = left_product(table(p, 0, 0), table(p, 0, 1), stacked)
        temp, salt = product[:, :half], product[:, half:]
        modulus = (sq_ref[:, p : p + 1] + sqt_ref[parity : parity + 1]) / (
            (length / 2.0) * (length / 2.0)
        )
        diag_temp = 1.0 + rate_t * modulus
        diag_salt = 1.0 + rate_s * modulus
        cross = rate_c * modulus
        determinant = diag_temp * diag_salt + cross * cross
        new_temp = (diag_salt * temp - cross * salt) / determinant
        new_salt = (diag_temp * salt + cross * temp) / determinant
        product = left_product(
            table(p, 1, 0), table(p, 1, 1), jnp.concatenate([new_temp, new_salt], axis=1)
        )
        for f in (0, 1):
            back[f, p] = product[:, f * half : (f + 1) * half]
    stacked = jnp.concatenate([back[f, p] for f in (0, 1) for p in (0, 1)], axis=0)
    result = right_product(stacked, table(parity, 0, 0), table(parity, 0, 1))
    out = []
    for f in (0, 1):
        plus = result[2 * f * half : (2 * f + 1) * half]
        minus = result[(2 * f + 1) * half : (2 * f + 2) * half]
        out.append((plus + minus, plus - minus))
    return out


def store_rows(out_ref, result):
    blocks, _, rows, half = out_ref.shape
    for f in (0, 1):
        for side in (0, 1):
            at = slice(side * blocks // 2, (side + 1) * blocks // 2)
            out_ref[at, f] = result[f][side].reshape(blocks // 2, rows, half)


def spectral_kernel(parity, rt_ref, rs_ref, rc_ref, tab_ref, sq_ref, sqt_ref, *refs):
    inputs, outs, held = (refs[:8], refs[8:12], refs[12]) if parity == 0 else (refs[:4], refs[4:12], refs[12])
    gathered(inputs, held)
    level = lax.axis_index("hor")
    rates = (rt_ref[level], rs_ref[level], rc_ref[level])
    store_rows(held, transformed(parity, rates, held, tab_ref, sq_ref, sqt_ref))
    place = position()
    for step in range(4):
        for near in range(8):
            block = held[block_to(place, step, near)]
            if parity == 0:
                outs[step][near] = block
            else:
                outs[near][step] = block


def unfolded(even, odd):
    return tuple(jnp.concatenate([even[f] + odd[f], even[f] - odd[f]], axis=-1) for f in (0, 1))


def face(lower, upper):
    lt, ls, lw = lower
    ut, us, uw = upper
    flow = 0.5 * (lw + uw) + buoyancy * 0.5 * ((lt + ut) - (ls + us))
    up = jnp.maximum(flow, 0.0)
    down = jnp.minimum(flow, 0.0)
    return up * lt + down * ut, up * ls + down * us


def inner_flux_kernel(even_ref, odd_ref, w_ref, t_out, s_out):
    levels = w_ref.shape[0]

    def at_level(level):
        return unfolded(even_ref[level], odd_ref[level]) + (w_ref[level],)

    at = at_level(0)
    below = (jnp.zeros_like(at[0]),) * 2

    def body(level, carried):
        at, below = carried[:3], carried[3:]
        nxt = at_level(level + 1)
        above = face(at, nxt)
        t_out[level] = at[0] - advective_number * (above[0] - below[0])
        s_out[level] = at[1] - advective_number * (above[1] - below[1])
        return nxt + above

    carried = at + below
    carried = lax.fori_loop(0, levels - 1, body, carried)
    at, below = carried[:3], carried[3:]
    t_out[levels - 1] = at[0] + advective_number * below[0]
    s_out[levels - 1] = at[1] + advective_number * below[1]


def outer_flux_kernel(t_ref, s_ref, first_ref, last_ref, low_ref, high_ref, t_out, s_out):
    block = lax.axis_index("lev")

    def fields(ref):
        return unfolded(ref[0:2], ref[2:4]) + (jnp.concatenate([ref[4], ref[5]], axis=-1),)

    def add(flux, sign, is_open):
        t_out[0] = t_ref[0] + sign * advective_number * jnp.where(is_open, flux[0], 0.0)
        s_out[0] = s_ref[0] + sign * advective_number * jnp.where(is_open, flux[1], 0.0)

    @pl.when(pl.program_id(0) == 0)
    def _():
        add(face(fields(low_ref), fields(first_ref)), 1.0, block > 0)

    @pl.when(pl.program_id(0) == 1)
    def _():
        add(face(fields(last_ref), fields(high_ref)), -1.0, block < lax.axis_size("lev") - 1)


def constants(length):
    tables, waves = real_basis(length)
    stack = []
    for table in tables:
        for oriented in (table, table.T):
            stack.extend(parts_of(oriented))
    squares = np.stack([w.astype(np.float32) ** 2 for w in waves], axis=1)
    return np.stack(stack), squares, np.ascontiguousarray(squares.T)


vmem = pl.BlockSpec(memory_space=pltpu.VMEM)
smem = pl.BlockSpec(memory_space=pltpu.SMEM)


def call(kernel, outs, *args, smem_args=0, scratch=(), flops=0, specs=None, grid=()):
    moved = sum(math.prod(a.shape) * 4 for a in args) + sum(math.prod(o.shape) * 4 for o in outs)
    return pl.pallas_call(
        kernel,
        out_shape=tuple(outs),
        grid=grid,
        in_specs=specs or [smem] * smem_args + [vmem] * (len(args) - smem_args),
        out_specs=(vmem,) * len(outs),
        scratch_shapes=scratch,
        compiler_params=pltpu.CompilerParams(vmem_limit_bytes=24 << 20),
        cost_estimate=pl.CostEstimate(flops=flops, bytes_accessed=moved, transcendentals=0),
    )(*args)


def step_of(heat, saline, updraft, rate_t, rate_s, rate_c):
    levels, rows, length = heat.shape
    half = length // 2
    f32 = jnp.float32
    by_plane = jax.ShapeDtypeStruct((8, 2, rows, half), f32)
    by_near = jax.ShapeDtypeStruct((4, 2, rows, half), f32)
    whole = jax.ShapeDtypeStruct((levels, 2, rows, half), f32)
    table, squares, squares_t = (jnp.asarray(c) for c in constants(length))
    shared = (rate_t, rate_s, rate_c, table, squares, squares_t)
    flops = 3 * 16 * 2 * half**3

    def along_z(pieces):
        out = [pieces[0]]
        for step in (1, 2, 3):
            pairs = [(h, (h + 8 * step) % 32) for h in range(32)]
            out.append(lax.ppermute(pieces[step], "hor", pairs))
        return out

    def in_plane(pieces):
        out = [pieces[0]]
        for near in range(1, 8):
            pairs = [
                (z * 8 + x * 2 + c, z * 8 + (x + near // 2) % 4 * 2 + (c + near) % 2)
                for z in range(4)
                for x in range(4)
                for c in range(2)
            ]
            out.append(lax.ppermute(pieces[near], "hor", pairs))
        return out

    def kernel(body, outs, *args, **kwargs):
        return call(body, outs, *args, **kwargs)

    def repacked(pieces):
        outs = [by_near] * 8 if len(pieces) == 4 else [by_plane] * 4
        return kernel(repack_kernel, outs, *pieces)

    def solved(parity, pieces):
        outs = [by_plane] * 4 if parity == 0 else [by_near] * 8
        return kernel(
            functools.partial(spectral_kernel, parity), outs, *shared, *pieces,
            smem_args=3, flops=flops, scratch=[pltpu.VMEM(whole.shape, f32)],
        )

    count = lax.axis_size("lev")
    upward = [(i, i + 1) for i in range(count - 1)]
    downward = [(i + 1, i) for i in range(count - 1)]

    folded = kernel(
        fold_kernel, [by_plane] * 4 + [by_near] * 8, heat, saline,
        specs=[pl.BlockSpec(memory_space=pltpu.HBM)] * 2,
        scratch=[pltpu.VMEM((2, 4, 8, rows, length), f32), pltpu.SemaphoreType.DMA((2, 4))],
    )
    even, odd = folded[:4], folded[4:]
    even = along_z(even)
    odd = in_plane(odd)
    odd = along_z(repacked(odd))
    even = in_plane(repacked(even))
    even = along_z(solved(0, even))
    odd = in_plane(solved(1, odd))
    odd = along_z(repacked(odd))
    even = in_plane(repacked(even))
    first_level = pl.BlockSpec((1, rows, length), lambda *_: (0, 0, 0))
    last_level = pl.BlockSpec((1, rows, length), lambda *_: (levels - 1, 0, 0))
    edge = jax.ShapeDtypeStruct((6, rows, half), f32)
    even, odd, *edges = kernel(
        unpack_kernel, [whole, whole, edge, edge], updraft, updraft, *even, *odd,
        specs=[first_level, last_level] + [vmem] * 12, grid=(1,),
    )
    low = lax.ppermute(edges[1], "lev", upward)
    high = lax.ppermute(edges[0], "lev", downward)
    field = jax.ShapeDtypeStruct(heat.shape, f32)
    temp, salt = kernel(inner_flux_kernel, [field, field], even, odd, updraft)
    in_field = pl.BlockSpec((1, rows, length), lambda i: (i * (levels - 1), 0, 0))
    in_edge = pl.BlockSpec((6, rows, half), lambda i: (0, 0, 0))
    return pl.pallas_call(
        outer_flux_kernel,
        grid=(2,),
        out_shape=(field, field),
        in_specs=[in_field] * 2 + [in_edge] * 4,
        out_specs=(in_field, in_field),
        input_output_aliases={0: 0, 1: 1},
        compiler_params=pltpu.CompilerParams(vmem_limit_bytes=60 << 20),
        name="outer",
    )(temp, salt, *edges, low, high)


def solution(mesh):
    field = P("lev", "hor", None)
    return jax.shard_map(
        step_of,
        mesh=mesh,
        in_specs=(field,) * 3 + (P("lev"),) * 3,
        out_specs=(field, field),
        check_vma=False,
    )
```
